32 devices in a mesh: lines: 4 (over y, x), buses: 8 (over z, core).
Axes of the slice: x: 2, y: 2, z: 4, core: 2. Of those that a mesh axis runs over, the one named last changes fastest.
Arguments:
- ptdf: bfloat16 [4096, 10240], P('lines', 'buses'), may hold values from -0.078125 to 0.078125
- load: float32 [384, 10240], P(None, 'buses'), may hold values from 0.03 to 3.8, as said below
- ratings: float32 [32768], replicated, may hold values from 0.3 to 3
- line_index: int32 [4096], P('lines'), may hold values from 0 to 32767
- gen_bus: int32 [2048], P('buses'), may hold values from 0 to 10239, as said below
- gen_quad: float32 [2048], P('buses'), may hold values from 0.05 to 0.5
- gen_lin: float32 [2048], P('buses'), may hold values from 0.5 to 2.5
- gen_max: float32 [2048], P('buses'), may hold values from 0.8 to 4
- gen_start: float32 [384, 2048], P(None, 'buses'), may hold values from 0 to 2
- stor_bus: int32 [1024], P('buses'), may hold values from 0 to 1279
- stor_quad: float32 [1024], P('buses'), may hold values from 0.05 to 0.5
- stor_rate: float32 [1024], P('buses'), may hold values from 0.3 to 1.5
- stor_energy: float32 [1024], P('buses'), may hold values from 1 to 8
- stor_start: float32 [384, 1024], P(None, 'buses'), may hold values from -0.5 to 0.5
- lam_start: float32 [384], replicated, may hold values from -4 to 4
- mu_start: float32 [384, 4096], P(None, ('lines', 'buses')), may hold values from -3 to 3
- omega_start: float32 [384, 1024], P(None, 'buses'), may hold values from -2 to 2
Outputs:
- gen_out: float32 [384, 2048], P(None, 'buses')
- stor_out: float32 [384, 1024], P(None, 'buses')
- lam_out: float32 [384], replicated
- mu_out: float32 [384, 4096], P(None, ('lines', 'buses'))
- omega_out: float32 [384, 1024], P(None, 'buses')
The draws below stay inside these ranges and needn't reach their ends.
Inputs may be any that keep to these rules, and one draw needn't show every extreme that they name: `gen_bus`: of the 256 generators of one area at most 32 sit on the buses of any one area (1280 consecutive buses); in every draw one area holds exactly 32 generators of every area, and the others of an area spread over the remaining areas as evenly as counts allow. `load`: loads are positive.
All inputs are finite; a program needn't handle non-finite values.
Results may differ from the reference program's by a relative error of at most 0.0075.
Values may be sent and summed in bfloat16 or wider, within the bound.
A program may use at most 64 MiB of HBM per device.

```python
import math
import jax
import jax.numpy as jnp

HOURS = 24
BUS_DEV = 1280
GEN_DEV = 256
STOR_DEV = 128
RATED = 32768
ROWS = 384
BUSES = 10240
LINES = 4096
GENS = 2048
STOR = 1024


def draw_load(key, part):
    area_count = BUSES // BUS_DEV
    bus_key, row_key, cell_key = jax.random.split(jax.random.fold_in(key, 11), 3)
    area_of = (jnp.arange(BUSES, dtype=jnp.int32) // BUS_DEV).astype(jnp.float32)
    rising = 1.0 + 2.0 * area_of / max(area_count - 1, 1)
    bus_factor = jax.random.uniform(bus_key, (BUSES,), jnp.float32, 0.5, 1.5)
    row_factor = jax.random.uniform(row_key, (ROWS, 1), jnp.float32, 0.7, 1.3)
    cell_factor = jax.random.uniform(cell_key, (ROWS, BUSES), jnp.float32, 0.8, 1.2)
    return (0.3 * rising[None, :] * bus_factor[None, :] * row_factor * cell_factor).astype(jnp.float32)


def draw_gen_bus(key, part):
    area_count = GENS // GEN_DEV
    slot_count = max(8, (GEN_DEV + area_count - 1) // area_count)
    hot_key, order_key, other_key, bus_key = jax.random.split(jax.random.fold_in(key, 23), 4)
    hot_area = jax.random.randint(hot_key, (), 0, area_count)
    position = jax.vmap(lambda sub_key: jax.random.permutation(sub_key, GEN_DEV))(jax.random.split(order_key, area_count))
    others = jax.vmap(lambda sub_key: jax.random.permutation(sub_key, area_count - 1))(jax.random.split(other_key, area_count))
    spill_index = jnp.maximum(position - slot_count, 0) % (area_count - 1)
    offset = jnp.take_along_axis(others, spill_index, axis=1)
    target = jnp.where(position < slot_count, hot_area, (hot_area + 1 + offset) % area_count)
    local_bus = jax.random.randint(bus_key, (area_count, GEN_DEV), 0, BUS_DEV)
    return (target * BUS_DEV + local_bus).reshape(GENS).astype(jnp.int32)


def plant(result, own_key, low, top_value):
    longest = result.shape.index(max(result.shape))
    spots = []
    for shift in (0, 1):
        where = [jax.random.randint(jax.random.fold_in(own_key, axis), (), 0, length) for axis, length in enumerate(result.shape)]
        where[longest] = (where[longest] + shift) % result.shape[longest]
        spots.append(tuple(where))
    return result.at[spots[0]].set(low).at[spots[1]].set(top_value)


def with_spikes(result, stream_key, source, target, parts, factor):
    def block_of(dim):
        return (jnp.arange(result.shape[dim]) // (result.shape[dim] // parts)).reshape((-1,) + (1,) * (result.ndim - 1 - dim))

    first = jax.random.permutation(stream_key, parts)[block_of(target)]
    other_side = (block_of(target) + parts // 2) % parts
    return jnp.where((block_of(source) == first) | (block_of(source) == other_side), factor * result, result)


def block_levels(key, shape, cuts, low, largest):
    def one(dim, parts):
        heights = jax.random.uniform(jax.random.fold_in(jax.random.fold_in(key, 6), dim), (parts,), jnp.float32, low / len(cuts), largest / len(cuts))
        return jnp.repeat(jnp.exp(heights), shape[dim] // parts).reshape((-1,) + (1,) * (len(shape) - dim - 1))

    factor_of = one(*cuts[0])
    for cut in cuts[1:]:
        factor_of = factor_of * one(*cut)
    return factor_of


def normal_values(stream_key, dims, deviation, most, shards=(), kind=jnp.bfloat16):
    factor_of = block_levels(stream_key, dims, shards, -0.22, 0.18) if shards else 1.0
    result = jax.random.normal(stream_key, dims, jnp.float32) * deviation * factor_of
    return jnp.minimum(jnp.maximum(result, -most), most).astype(kind)


def bell_draw_with(own_key, dims, spread, reach, cuts, heavy, kind=jnp.bfloat16):
    result = spread * jax.random.normal(own_key, dims, jnp.float32)
    if cuts:
        result = result * block_levels(own_key, dims, cuts, -0.22, 0.18)
    return jnp.clip(with_spikes(result, jax.random.fold_in(own_key, 3), *heavy), -reach, reach).astype(kind)


def setup_inputs(seed: int = 0) -> dict:
    splits = jax.random.split(jax.random.key(seed), 18)
    ptdf = bell_draw_with(splits[0], (LINES, BUSES), BUSES ** -0.5, 0.078125, ((0, 4), (1, 8)), (1, 0, 8, 2.0))
    load = draw_load(jax.random.fold_in(splits[17], 71), 0)
    ratings = jnp.clip(jnp.exp(jax.random.uniform(splits[2], (RATED,), jnp.float32, math.log(0.3), math.log(3.0))), 0.3, 3.0)
    line_index = plant(jax.random.randint(splits[3], (LINES,), 0, RATED), jax.random.fold_in(splits[3], 1), 0, RATED - 1).astype(jnp.int32)
    gen_bus = draw_gen_bus(jax.random.fold_in(splits[17], 71), 0)
    gen_quad = jnp.clip(jnp.exp(math.log(0.5) - 2.3025851 * jax.random.uniform(splits[5], (GENS,), jnp.float32) ** block_levels(splits[5], (GENS,), ((0, 8),), -0.2, 0.2)), 0.05, 0.5)
    gen_lin = jnp.clip(0.5 + 2.0 * jax.random.uniform(splits[6], (GENS,), jnp.float32) ** block_levels(splits[6], (GENS,), ((0, 8),), -0.2, 0.2), 0.5, 2.5)
    gen_max = jnp.clip(jnp.exp(math.log(4.0) - 1.609438 * jax.random.uniform(splits[7], (GENS,), jnp.float32) ** block_levels(splits[7], (GENS,), ((0, 8),), -0.2, 0.2)), 0.8, 4.0)
    gen_start = jnp.clip(2.0 * jax.random.uniform(splits[8], (ROWS, GENS), jnp.float32) ** block_levels(splits[8], (ROWS, GENS), ((1, 8),), -0.2, 0.2), 0.0, 2.0)
    stor_bus = plant(jax.random.randint(splits[9], (STOR,), 0, BUS_DEV), jax.random.fold_in(splits[9], 1), 0, BUS_DEV - 1).astype(jnp.int32)
    stor_quad = jnp.clip(jnp.exp(math.log(0.5) - 2.3025851 * jax.random.uniform(splits[10], (STOR,), jnp.float32) ** block_levels(splits[10], (STOR,), ((0, 8),), -0.2, 0.2)), 0.05, 0.5)
    stor_rate = jnp.clip(jnp.exp(math.log(1.5) - 1.60943787 * jax.random.uniform(splits[11], (STOR,), jnp.float32) ** block_levels(splits[11], (STOR,), ((0, 8),), -0.2, 0.2)), 0.3, 1.5)
    stor_energy = jnp.clip(jnp.exp(math.log(8.0) - 2.0794415 * jax.random.uniform(splits[12], (STOR,), jnp.float32) ** block_levels(splits[12], (STOR,), ((0, 8),), -0.2, 0.2)), 1.0, 8.0)
    stor_start = jnp.clip(jax.random.uniform(splits[13], (ROWS, STOR), jnp.float32, -0.5, 0.5) * block_levels(splits[13], (ROWS, STOR), ((1, 8),), -0.4, 0.0), -0.5, 0.5)
    lam_start = normal_values(splits[14], (ROWS,), 1.0, 4.0, (), jnp.float32)
    mu_start = normal_values(splits[15], (ROWS, LINES), 0.5, 3.0, ((1, 32),), jnp.float32)
    omega_start = normal_values(splits[16], (ROWS, STOR), 0.3, 2.0, ((1, 8),), jnp.float32)
    return dict(ptdf=ptdf, load=load, ratings=ratings, line_index=line_index, gen_bus=gen_bus, gen_quad=gen_quad, gen_lin=gen_lin, gen_max=gen_max, gen_start=gen_start, stor_bus=stor_bus, stor_quad=stor_quad, stor_rate=stor_rate, stor_energy=stor_energy, stor_start=stor_start, lam_start=lam_start, mu_start=mu_start, omega_start=omega_start)


TAU = 0.25
SIGMA_FLOW = 4.0
SIGMA_STORE = 0.25
KAPPA = 1.0
THETA = 0.5


def reverse_cum(values, hour_count):
    total_rows, columns = values.shape
    shaped = values.reshape(total_rows // hour_count, hour_count, columns)
    summed = jnp.flip(jnp.cumsum(jnp.flip(shaped, 1), axis=1), 1)
    return summed.reshape(total_rows, columns)


def forward_cum(values, hour_count):
    total_rows, columns = values.shape
    shaped = values.reshape(total_rows // hour_count, hour_count, columns)
    return jnp.cumsum(shaped, axis=1).reshape(total_rows, columns)


def dual_step(dual_now, image_term, step_size, low_bound, high_bound):
    shifted = dual_now + step_size * image_term
    return shifted - step_size * jnp.clip(shifted / step_size, low_bound, high_bound)


def reference(ptdf, load, ratings, line_index, gen_bus, gen_quad, gen_lin, gen_max, gen_start,
              stor_bus, stor_quad, stor_rate, stor_energy, stor_start, lam_start, mu_start, omega_start):
    stor_global = (jnp.arange(STOR, dtype=jnp.int32) // STOR_DEV) * BUS_DEV + stor_bus.astype(jnp.int32)
    gen_index = gen_bus.astype(jnp.int32)
    limit = jnp.take(ratings, line_index.astype(jnp.int32))
    hour_of = jnp.arange(ROWS, dtype=jnp.int32) % HOURS
    last_hour = (hour_of == HOURS - 1)[:, None]
    half_energy = (0.5 * stor_energy)[None, :]
    low_bound = jnp.where(last_hour, jnp.zeros_like(half_energy), -half_energy)
    high_bound = jnp.where(last_hour, jnp.zeros_like(half_energy), half_energy)
    load_total = jnp.sum(load, axis=1)
    gen_now, stor_now = gen_start, stor_start
    gen_old, stor_old = gen_start, stor_start
    price_level, dual_flow, dual_store = lam_start, mu_start, omega_start
    for iteration in range(2):
        if iteration == 0:
            gen_mid, stor_mid = gen_now, stor_now
        else:
            gen_mid = gen_now + THETA * (gen_now - gen_old)
            stor_mid = stor_now + THETA * (stor_now - stor_old)
        bus_price = jnp.dot(dual_flow.astype(jnp.bfloat16), ptdf, preferred_element_type=jnp.float32)
        gen_price = jnp.take(bus_price, gen_index, axis=1)
        stor_price = jnp.take(bus_price, stor_global, axis=1)
        gen_grad = 2.0 * gen_quad * gen_mid + gen_lin + price_level[:, None] + gen_price
        gen_next = jnp.clip(gen_mid - TAU * gen_grad, 0.0, gen_max)
        stor_grad = 2.0 * stor_quad * stor_mid + price_level[:, None] + stor_price + reverse_cum(dual_store, HOURS)
        stor_next = jnp.clip(stor_mid - TAU * stor_grad, -stor_rate, stor_rate)
        gen_bar = 2.0 * gen_next - gen_now
        stor_bar = 2.0 * stor_next - stor_now
        gen_inject = jax.ops.segment_sum(gen_bar.T, gen_index, num_segments=BUSES).T
        stor_inject = jax.ops.segment_sum(stor_bar.T, stor_global, num_segments=BUSES).T
        injection = gen_inject + stor_inject - load
        flow_sum = jnp.dot(injection.astype(jnp.bfloat16), ptdf.T, preferred_element_type=jnp.float32)
        dual_flow = dual_step(dual_flow, flow_sum, SIGMA_FLOW, -limit, limit)
        balance = jnp.sum(gen_bar, axis=1) + jnp.sum(stor_bar, axis=1) - load_total
        price_level = price_level + (KAPPA / (GENS + STOR)) * balance
        dual_store = dual_step(dual_store, forward_cum(stor_bar, HOURS), SIGMA_STORE, low_bound, high_bound)
        gen_old, stor_old = gen_now, stor_now
        gen_now, stor_now = gen_next, stor_next
    return gen_now, stor_now, price_level, dual_flow, dual_store
```

```python
import functools
import jax
import jax.numpy as jnp
from jax import lax
from jax.experimental import pallas as pl
from jax.experimental.pallas import tpu as pltpu
from jax.sharding import PartitionSpec as P

HOURS = 24
TAU = 0.25
SIGMA_FLOW = 4.0
SIGMA_STORE = 0.25
KAPPA = 1.0
THETA = 0.5

F32 = jnp.float32
BF16 = jnp.bfloat16
MESH = pl.DeviceIdType.MESH
HIGHEST = lax.Precision.HIGHEST


def nt(a, b, precision=None):
    return lax.dot_general(
        a, b, (((1,), (1,)), ((), ())), preferred_element_type=F32, precision=precision
    )


def nn(a, b, precision=None):
    return lax.dot_general(
        a, b, (((1,), (0,)), ((), ())), preferred_element_type=F32, precision=precision
    )


def iota(shape, dim):
    return lax.broadcasted_iota(jnp.int32, shape, dim)


def eye(n):
    return iota((n, n), 0) == iota((n, n), 1)


def flipped(x):
    return nt(eye(x.shape[1]).astype(F32), x, HIGHEST)


def to_column(row):
    n = row.shape[1]
    return jnp.sum(jnp.where(eye(n), row, 0.0), axis=1, keepdims=True)


def to_row(column):
    n = column.shape[0]
    return jnp.sum(jnp.where(eye(n), column, 0.0), axis=0, keepdims=True)


def remote(src, dst, send_sem, recv_sem, target):
    return pltpu.make_async_remote_copy(
        src_ref=src,
        dst_ref=dst,
        send_sem=send_sem,
        recv_sem=recv_sem,
        device_id=target,
        device_id_type=MESH,
    )


def kernel(
    lines_n,
    buses_n,
    slots,
    gen_bus,
    mu_in,
    ratings,
    line_index,
    gen_quad,
    gen_lin,
    gen_max,
    gen_start,
    stor_bus,
    stor_quad,
    stor_rate,
    stor_energy,
    stor_start,
    lam_in,
    omega_in,
    ptdf_hbm,
    load_hbm,
    gen_out,
    stor_out,
    lam_out,
    mu_out,
    omega_out,
    ptdf,
    load,
    load_low,
    load_flow,
    gen_all,
    a_send,
    a_recv,
    a_t,
    a_n,
    dual_all,
    price_part,
    price_recv,
    price_all,
    bar_low,
    flow_part,
    pair_recv,
    line_part,
    line_recv,
    bal_send,
    bal_recv,
    in_sem,
    idx_sem,
    a_sem,
    ag_sem,
    fwd_sem,
    pr_sem,
    pg_sem,
    pair_sem,
    line_sem,
    bal_sem,
):
    rows = load.shape[0]
    line_count, bus_count = ptdf.shape
    gens = gen_bus.shape[1]
    stors = stor_bus.shape[1]
    units = gens + stors
    share = mu_in.shape[1]
    chips = buses_n // 2
    width = buses_n * slots
    piece = units // lines_n
    i = lax.axis_index("lines")
    j = lax.axis_index("buses")
    z = j // 2
    c = j % 2
    partner = (i, z * 2 + (1 - c))

    load_copy = pltpu.make_async_copy(load_hbm, load, in_sem.at[0])
    ptdf_copy = pltpu.make_async_copy(ptdf_hbm, ptdf, in_sem.at[1])
    load_copy.start()
    ptdf_copy.start()

    barrier = pltpu.get_barrier_semaphore()
    for off in range(1, buses_n):
        pl.semaphore_signal(
            barrier, inc=1, device_id=(i, lax.rem(j + off, buses_n)), device_id_type=MESH
        )
    for off in range(1, lines_n):
        pl.semaphore_signal(
            barrier, inc=1, device_id=(lax.rem(i + off, lines_n), j), device_id_type=MESH
        )

    gen_all[j] = gen_bus[...]
    mu = flipped(mu_in[...])
    dual_all[0, j] = mu.astype(BF16)
    pl.semaphore_wait(barrier, buses_n + lines_n - 2)

    started = []

    def go(copy):
        copy.start()
        started.append(copy)
        return copy

    idx_copies = []
    for off in range(1, buses_n):
        idx_copies.append(
            go(
                remote(
                    gen_bus,
                    gen_all.at[j],
                    idx_sem.at[0, off],
                    idx_sem.at[1, off],
                    (i, lax.rem(j + off, buses_n)),
                )
            )
        )

    def gather_start(k):
        mine = dual_all.at[k, j]
        copies = [go(remote(mine, mine, ag_sem.at[k, 0, 0], ag_sem.at[k, 1, 0], partner))]
        for off in range(1, chips):
            copies.append(
                go(
                    remote(
                        mine,
                        mine,
                        ag_sem.at[k, 0, off],
                        ag_sem.at[k, 1, off],
                        (i, lax.rem(z + off, chips) * 2 + c),
                    )
                )
            )
        return copies

    def gather_finish(k, copies):
        forwards = []
        for off in range(1, chips):
            copies[off].wait_recv()
            slot = dual_all.at[k, lax.rem(z - off + chips, chips) * 2 + c]
            forwards.append(
                go(remote(slot, slot, fwd_sem.at[k, 0, off], fwd_sem.at[k, 1, off], partner))
            )
        copies[0].wait_recv()
        for copy in forwards:
            copy.wait_recv()

    gather = gather_start(0)

    load_copy.wait()
    load_value = load[...]
    load_total = jnp.sum(load_value, axis=1, keepdims=True)
    load_low[...] = load_value.astype(BF16)
    lam = to_column(lam_in[...])
    wanted = jnp.sum(
        jnp.where(iota((buses_n, share), 0) == j, line_index[...].astype(F32), 0.0),
        axis=0,
        keepdims=True,
    )
    wanted = to_column(wanted).astype(jnp.int32)
    lanes = ratings.shape[1]
    high_hit = (iota((share, ratings.shape[0]), 1) == wanted // lanes).astype(F32)
    rated = nn(high_hit, ratings[...], HIGHEST)
    limit = jnp.sum(
        jnp.where(iota((share, lanes), 1) == wanted % lanes, rated, 0.0), axis=1, keepdims=True
    )
    hour = iota((rows, 1), 0) % HOURS
    half_energy = 0.5 * stor_energy[...]
    high_bound = jnp.where(hour == HOURS - 1, 0.0, half_energy)
    row_id, col_id = (iota((rows, rows), 0), iota((rows, rows), 1))
    same = row_id // HOURS == col_id // HOURS
    later = jnp.where(same & (col_id >= row_id), 1.0, 0.0)
    earlier = jnp.where(same & (col_id <= row_id), 1.0, 0.0)

    for copy in idx_copies:
        copy.wait_recv()
    ids = jnp.concatenate([gen_all[a] for a in range(buses_n)], axis=0)
    ids = flipped(ids.astype(F32)).astype(jnp.int32)
    local = ids - j * bus_count
    hit = (local >= 0) & (local < bus_count)
    upto = (iota((gens, gens), 1) <= iota((gens, gens), 0)).astype(BF16)
    rank = nn(upto, hit.astype(BF16)) - 1.0
    rank = jnp.where(hit, rank, 512.0)
    local = jnp.where(hit, local, 0)
    spread = (iota((buses_n, width), 1) // slots == iota((buses_n, width), 0)).astype(BF16)
    rank_wide = nn(rank.astype(BF16), spread)
    high_wide = nn((local // 128).astype(BF16), spread)
    low_wide = nn((local % 128).astype(BF16), spread)
    taken = rank_wide == (iota((gens, width), 1) % slots).astype(F32)
    slot_bus = jnp.sum(jnp.where(taken, high_wide * 128.0 + low_wide + 1.0, 0.0), axis=0, keepdims=True)
    slot_bus = to_column(slot_bus).astype(jnp.int32) - 1
    slot_hit = (iota((width, bus_count), 1) == slot_bus).astype(BF16)
    stor_column = to_column(stor_bus[...].astype(F32)).astype(jnp.int32)
    stor_hit = (iota((stors, bus_count), 1) == stor_column).astype(BF16)
    ptdf_copy.wait()
    tile = 128

    def columns_step(t, carry):
        at = pl.multiple_of(t * tile, tile)
        block = ptdf[pl.ds(at, tile), :]
        a_send[:, :, pl.ds(at, tile)] = nt(slot_hit, block).astype(BF16).reshape(buses_n, slots, tile)
        return carry

    lax.fori_loop(0, line_count // tile, columns_step, 0)
    a_recv[j] = a_send[j]
    a_copies = []
    for off in range(1, buses_n):
        to = lax.rem(j + off, buses_n)
        a_copies.append(
            go(remote(a_send.at[to], a_recv.at[j], a_sem.at[0, off], a_sem.at[1, off], (i, to)))
        )

    def load_step(t, carry):
        at = pl.multiple_of(t * tile, tile)
        block = ptdf[pl.ds(at, tile), :]
        load_flow[pl.ds(at, tile), :] = nt(block, load_low[...])
        stor_block = nt(block, stor_hit)
        a_n[pl.ds(at, tile), gens:] = stor_block.astype(BF16)
        a_t[gens:, pl.ds(at, tile)] = stor_block.T.astype(BF16)
        return carry

    lax.fori_loop(0, line_count // tile, load_step, 0)
    own = jnp.sum(jnp.where(iota((gens, buses_n), 1) == j, ids, 0), axis=1, keepdims=True)
    target = own // bus_count
    target_hit = iota((gens, buses_n), 1) == target
    own_rank = nn(upto, target_hit.astype(BF16))
    own_rank = jnp.sum(jnp.where(target_hit, own_rank, 0.0), axis=1, keepdims=True).astype(jnp.int32) - 1
    place = (iota((gens, width), 1) == target * slots + own_rank).astype(BF16)

    gather_finish(0, gather)
    for copy in a_copies:
        copy.wait_recv()

    def place_step(t, carry):
        at = pl.multiple_of(t * tile, tile)
        block = nn(place, a_recv[:, :, pl.ds(at, tile)].reshape(width, tile))
        a_t[:gens, pl.ds(at, tile)] = block.astype(BF16)
        a_n[pl.ds(at, tile), :gens] = block.T.astype(BF16)
        return carry

    lax.fori_loop(0, line_count // tile, place_step, 0)

    gen_now, stor_now = (gen_start[...], stor_start[...])
    gen_old, stor_old = (gen_now, stor_now)
    omega = omega_in[...]
    total_units = units * buses_n
    for k in range(2):
        if k == 0:
            gen_mid, stor_mid = (gen_now, stor_now)
        else:
            gen_mid = gen_now + THETA * (gen_now - gen_old)
            stor_mid = stor_now + THETA * (stor_now - stor_old)
        duals = dual_all[k].reshape(line_count, rows)
        copies = []
        for off in range(1, lines_n + 1):
            to = lax.rem(i + off, lines_n)
            at = pl.multiple_of(to * piece, piece)
            value = nn(a_t[pl.ds(at, piece), :], duals)
            if off == lines_n:
                total = value
                break
            price_part[k, off] = value.astype(BF16)
            copies.append(
                go(
                    remote(
                        price_part.at[k, off],
                        price_recv.at[k, off],
                        pr_sem.at[k, 0, off],
                        pr_sem.at[k, 1, off],
                        (to, j),
                    )
                )
            )
        back = nn(later, omega, HIGHEST)
        for off in range(1, lines_n):
            copies[off - 1].wait_recv()
            total = total + price_recv[k, off].astype(F32)
        price_all[k, i] = total.astype(BF16)
        copies = []
        for off in range(1, lines_n):
            copies.append(
                go(
                    remote(
                        price_all.at[k, i],
                        price_all.at[k, i],
                        pg_sem.at[k, 0, off],
                        pg_sem.at[k, 1, off],
                        (lax.rem(i + off, lines_n), j),
                    )
                )
            )
        for copy in copies:
            copy.wait_recv()
        price = price_all[k].reshape(units, rows).astype(F32).T

        gen_grad = 2.0 * gen_quad[...] * gen_mid + gen_lin[...] + lam + price[:, :gens]
        gen_next = jnp.clip(gen_mid - TAU * gen_grad, 0.0, gen_max[...])
        stor_grad = 2.0 * stor_quad[...] * stor_mid + lam + price[:, gens:] + back
        stor_next = jnp.clip(stor_mid - TAU * stor_grad, -stor_rate[...], stor_rate[...])
        gen_bar = 2.0 * gen_next - gen_now
        stor_bar = 2.0 * stor_next - stor_now
        bar_low[:, :gens] = gen_bar.astype(BF16)
        bar_low[:, gens:] = stor_bar.astype(BF16)

        def flow_step(chip, carry, want):
            at = pl.multiple_of((chip * 2 + want) * share, share)
            value = nt(a_n[pl.ds(at, share), :], bar_low[...]) - load_flow[pl.ds(at, share), :]
            flow_part[k, want, chip] = value.astype(BF16)
            return carry

        lax.fori_loop(0, chips, functools.partial(flow_step, want=1 - c), 0)
        pair_copy = go(
            remote(
                flow_part.at[k, 1 - c],
                pair_recv.at[k],
                pair_sem.at[k, 0],
                pair_sem.at[k, 1],
                partner,
            )
        )
        lax.fori_loop(0, chips, functools.partial(flow_step, want=c), 0)
        pair_copy.wait_recv()
        copies = []
        for off in range(1, chips):
            to = lax.rem(z + off, chips)
            line_part[k, off] = (flow_part[k, c, to].astype(F32) + pair_recv[k, to].astype(F32)).astype(BF16)
            copies.append(
                go(
                    remote(
                        line_part.at[k, off],
                        line_recv.at[k, off],
                        line_sem.at[k, 0, off],
                        line_sem.at[k, 1, off],
                        (i, to * 2 + c),
                    )
                )
            )
        balance = (
            jnp.sum(gen_bar, axis=1, keepdims=True)
            + jnp.sum(stor_bar, axis=1, keepdims=True)
            - load_total
        )
        balance = to_row(balance)
        bal_send[k] = balance
        bal_copies = []
        for off in range(1, buses_n):
            bal_copies.append(
                go(
                    remote(
                        bal_send.at[k],
                        bal_recv.at[k, j],
                        bal_sem.at[k, 0, off],
                        bal_sem.at[k, 1, off],
                        (i, lax.rem(j + off, buses_n)),
                    )
                )
            )
        bal_recv[k, j] = balance
        charge = nn(earlier, stor_bar, HIGHEST)
        shifted = omega + SIGMA_STORE * charge
        omega = shifted - SIGMA_STORE * jnp.clip(shifted / SIGMA_STORE, -high_bound, high_bound)
        flow = flow_part[k, c, z].astype(F32) + pair_recv[k, z].astype(F32)
        for off in range(1, chips):
            copies[off - 1].wait_recv()
            flow = flow + line_recv[k, off].astype(F32)
        shifted = mu + SIGMA_FLOW * flow
        mu = shifted - SIGMA_FLOW * jnp.clip(shifted / SIGMA_FLOW, -limit, limit)
        if k == 0:
            dual_all[1, j] = mu.astype(BF16)
            gather = gather_start(1)
        gen_old, stor_old = (gen_now, stor_now)
        gen_now, stor_now = (gen_next, stor_next)
        for copy in bal_copies:
            copy.wait_recv()
        balance = bal_recv[k, 0]
        for a in range(1, buses_n):
            balance = balance + bal_recv[k, a]
        lam = lam + (KAPPA / total_units) * to_column(balance)
        if k == 0:
            gather_finish(1, gather)

    gen_out[...] = gen_now
    stor_out[...] = stor_now
    lam_out[...] = to_row(lam)
    mu_out[...] = flipped(mu)
    omega_out[...] = omega
    for copy in started:
        copy.wait_send()


def shards(
    ptdf,
    load,
    ratings,
    line_index,
    gen_bus,
    gen_quad,
    gen_lin,
    gen_max,
    gen_start,
    stor_bus,
    stor_quad,
    stor_rate,
    stor_energy,
    stor_start,
    lam_start,
    mu_start,
    omega_start,
):
    lines_n = lax.axis_size("lines")
    buses_n = lax.axis_size("buses")
    rows, bus_count = load.shape
    line_count = ptdf.shape[0]
    gens = gen_bus.shape[0]
    stors = stor_bus.shape[0]
    units = gens + stors
    share = line_count // buses_n
    chips = buses_n // 2
    piece = units // lines_n
    slots = max(8, (gens + buses_n - 1) // buses_n)
    slots = (slots + 15) // 16 * 16
    width = buses_n * slots
    vmem = pl.BlockSpec(memory_space=pltpu.VMEM)
    hbm = pl.BlockSpec(memory_space=pl.ANY)
    dma = pltpu.SemaphoreType.DMA
    outs = pl.pallas_call(
        functools.partial(kernel, lines_n, buses_n, slots),
        out_shape=(
            jax.ShapeDtypeStruct((rows, gens), F32),
            jax.ShapeDtypeStruct((rows, stors), F32),
            jax.ShapeDtypeStruct((1, rows), F32),
            jax.ShapeDtypeStruct((rows, share), F32),
            jax.ShapeDtypeStruct((rows, stors), F32),
        ),
        in_specs=[vmem] * 15 + [hbm] * 2,
        out_specs=(vmem,) * 5,
        scratch_shapes=[
            pltpu.VMEM((line_count, bus_count), BF16),
            pltpu.VMEM((rows, bus_count), F32),
            pltpu.VMEM((rows, bus_count), BF16),
            pltpu.VMEM((line_count, rows), F32),
            pltpu.VMEM((buses_n, 1, gens), jnp.int32),
            pltpu.VMEM((buses_n, slots, line_count), BF16),
            pltpu.VMEM((buses_n, slots, line_count), BF16),
            pltpu.VMEM((units, line_count), BF16),
            pltpu.VMEM((line_count, units), BF16),
            pltpu.VMEM((2, buses_n, share, rows), BF16),
            pltpu.VMEM((2, lines_n, piece, rows), BF16),
            pltpu.VMEM((2, lines_n, piece, rows), BF16),
            pltpu.VMEM((2, lines_n, piece, rows), BF16),
            pltpu.VMEM((rows, units), BF16),
            pltpu.VMEM((2, 2, chips, share, rows), BF16),
            pltpu.VMEM((2, chips, share, rows), BF16),
            pltpu.VMEM((2, chips, share, rows), BF16),
            pltpu.VMEM((2, chips, share, rows), BF16),
            pltpu.VMEM((2, 1, rows), F32),
            pltpu.VMEM((2, buses_n, 1, rows), F32),
            dma((2,)),
            dma((2, buses_n)),
            dma((2, buses_n)),
            dma((2, 2, chips)),
            dma((2, 2, chips)),
            dma((2, 2, lines_n)),
            dma((2, 2, lines_n)),
            dma((2, 2)),
            dma((2, 2, chips)),
            dma((2, 2, buses_n)),
        ],
        compiler_params=pltpu.CompilerParams(
            collective_id=0, has_side_effects=True, vmem_limit_bytes=60 * 1024 * 1024
        ),
    )(
        gen_bus[None, :],
        mu_start,
        ratings.reshape(-1, 128),
        line_index.reshape(buses_n, share),
        gen_quad[None, :],
        gen_lin[None, :],
        gen_max[None, :],
        gen_start,
        stor_bus[None, :],
        stor_quad[None, :],
        stor_rate[None, :],
        stor_energy[None, :],
        stor_start,
        lam_start[None, :],
        omega_start,
        ptdf,
        load,
    )
    return (outs[0], outs[1], outs[2].reshape(rows), outs[3], outs[4])


def solution(mesh):
    return jax.shard_map(
        shards,
        mesh=mesh,
        in_specs=(
            P("lines", "buses"),
            P(None, "buses"),
            P(),
            P("lines"),
            P("buses"),
            P("buses"),
            P("buses"),
            P("buses"),
            P(None, "buses"),
            P("buses"),
            P("buses"),
            P("buses"),
            P("buses"),
            P(None, "buses"),
            P(),
            P(None, ("lines", "buses")),
            P(None, "buses"),
        ),
        out_specs=(
            P(None, "buses"),
            P(None, "buses"),
            P(),
            P(None, ("lines", "buses")),
            P(None, "buses"),
        ),
        check_vma=False,
    )
```

```python
import functools
import jax
import jax.numpy as jnp
from jax import lax
from jax.experimental import pallas as pl
from jax.experimental.pallas import tpu as pltpu
from jax.sharding import PartitionSpec as P

HOURS = 24
TAU = 0.25
SIGMA_FLOW = 4.0
SIGMA_STORE = 0.25
KAPPA = 1.0
THETA = 0.5

F32 = jnp.float32
BF16 = jnp.bfloat16
MESH = pl.DeviceIdType.MESH
HIGHEST = lax.Precision.HIGHEST


def nt(a, b, precision=None):
    return lax.dot_general(
        a, b, (((1,), (1,)), ((), ())), preferred_element_type=F32, precision=precision
    )


def nn(a, b, precision=None):
    return lax.dot_general(
        a, b, (((1,), (0,)), ((), ())), preferred_element_type=F32, precision=precision
    )


def iota(shape, dim):
    return lax.broadcasted_iota(jnp.int32, shape, dim)


def eye(n):
    return iota((n, n), 0) == iota((n, n), 1)


def flipped(x):
    return nt(eye(x.shape[1]).astype(F32), x, HIGHEST)


def to_column(row):
    n = row.shape[1]
    return jnp.sum(jnp.where(eye(n), row, 0.0), axis=1, keepdims=True)


def to_row(column):
    n = column.shape[0]
    return jnp.sum(jnp.where(eye(n), column, 0.0), axis=0, keepdims=True)


def remote(src, dst, send_sem, recv_sem, target):
    return pltpu.make_async_remote_copy(
        src_ref=src,
        dst_ref=dst,
        send_sem=send_sem,
        recv_sem=recv_sem,
        device_id=target,
        device_id_type=MESH,
    )


def kernel(
    lines_n,
    buses_n,
    slots,
    gen_bus,
    mu_in,
    ratings,
    line_index,
    gen_quad,
    gen_lin,
    gen_max,
    gen_start,
    stor_bus,
    stor_quad,
    stor_rate,
    stor_energy,
    stor_start,
    lam_in,
    omega_in,
    ptdf_hbm,
    load_hbm,
    gen_out,
    stor_out,
    lam_out,
    mu_out,
    omega_out,
    ptdf,
    load,
    load_low,
    load_flow,
    gen_all,
    a_send,
    a_recv,
    a_t,
    a_n,
    dual_all,
    price_part,
    price_recv,
    price_all,
    gen_keep,
    stor_keep,
    bar_keep,
    flow_part,
    pair_recv,
    line_part,
    line_recv,
    bal_send,
    bal_recv,
    in_sem,
    idx_sem,
    a_sem,
    ag_sem,
    fwd_sem,
    pr_sem,
    pg_sem,
    pair_sem,
    line_sem,
    bal_sem,
):
    rows = load.shape[0]
    line_count, bus_count = ptdf.shape
    gens = gen_bus.shape[1]
    stors = stor_bus.shape[1]
    units = gens + stors
    share = mu_in.shape[1]
    chips = buses_n // 2
    width = buses_n * slots
    piece = units // lines_n
    i = lax.axis_index("lines")
    j = lax.axis_index("buses")
    z = j // 2
    c = j % 2
    partner = (i, z * 2 + (1 - c))
    chunk = dual_all.shape[-1]
    chunks = rows // chunk

    def cut(n):
        return slice(n * chunk, (n + 1) * chunk)


    load_copy = pltpu.make_async_copy(load_hbm, load, in_sem.at[0])
    ptdf_copy = pltpu.make_async_copy(ptdf_hbm, ptdf, in_sem.at[1])
    load_copy.start()
    ptdf_copy.start()

    barrier = pltpu.get_barrier_semaphore()
    for off in range(1, buses_n):
        pl.semaphore_signal(
            barrier, inc=1, device_id=(i, lax.rem(j + off, buses_n)), device_id_type=MESH
        )
    for off in range(1, lines_n):
        pl.semaphore_signal(
            barrier, inc=1, device_id=(lax.rem(i + off, lines_n), j), device_id_type=MESH
        )

    gen_all[j] = gen_bus[...]
    mu = flipped(mu_in[...])
    for n in range(chunks):
        dual_all[0, n, j] = mu[:, cut(n)].astype(BF16)
    pl.semaphore_wait(barrier, buses_n + lines_n - 2)

    started = []

    def go(copy):
        copy.start()
        started.append(copy)
        return copy

    idx_copies = []
    for off in range(1, buses_n):
        idx_copies.append(
            go(
                remote(
                    gen_bus,
                    gen_all.at[j],
                    idx_sem.at[0, off],
                    idx_sem.at[1, off],
                    (i, lax.rem(j + off, buses_n)),
                )
            )
        )

    def gather_start(k, n):
        mine = dual_all.at[k, n, j]
        copies = []
        for off in range(1, chips):
            copies.append(
                go(
                    remote(
                        mine,
                        mine,
                        ag_sem.at[k, n, 0, off],
                        ag_sem.at[k, n, 1, off],
                        (i, lax.rem(z + off, chips) * 2 + c),
                    )
                )
            )
        copies.append(go(remote(mine, mine, ag_sem.at[k, n, 0, 0], ag_sem.at[k, n, 1, 0], partner)))
        return copies

    def gather_forward(k, n, copies):
        forwards = [copies[-1]]
        for off in range(1, chips):
            copies[off - 1].wait_recv()
            slot = dual_all.at[k, n, lax.rem(z - off + chips, chips) * 2 + c]
            forwards.append(
                go(remote(slot, slot, fwd_sem.at[k, n, 0, off], fwd_sem.at[k, n, 1, off], partner))
            )
        return forwards

    gather = [gather_start(0, n) for n in range(chunks)]

    load_copy.wait()
    load_value = load[...]
    load_total = jnp.sum(load_value, axis=1, keepdims=True)
    load_low[...] = load_value.astype(BF16)
    lam_row = lam_in[...].reshape(1, rows)
    lam = [to_column(lam_row[:, cut(n)]) for n in range(chunks)]
    wanted = jnp.sum(
        jnp.where(iota((buses_n, share), 0) == j, line_index[...].astype(F32), 0.0),
        axis=0,
        keepdims=True,
    )
    wanted = to_column(wanted).astype(jnp.int32)
    lanes = ratings.shape[1]
    high_hit = (iota((share, ratings.shape[0]), 1) == wanted // lanes).astype(F32)
    rated = nn(high_hit, ratings[...], HIGHEST)
    limit = jnp.sum(
        jnp.where(iota((share, lanes), 1) == wanted % lanes, rated, 0.0), axis=1, keepdims=True
    )
    hour = iota((rows, 1), 0) % HOURS
    half_energy = 0.5 * stor_energy[...]
    high_bound = jnp.where(hour == HOURS - 1, 0.0, half_energy)
    row_id, col_id = (iota((rows, rows), 0), iota((rows, rows), 1))
    same = row_id // HOURS == col_id // HOURS
    later = jnp.where(same & (col_id >= row_id), 1.0, 0.0)
    earlier = jnp.where(same & (col_id <= row_id), 1.0, 0.0)

    for copy in idx_copies:
        copy.wait_recv()
    ids = jnp.concatenate([gen_all[a] for a in range(buses_n)], axis=0)
    ids = flipped(ids.astype(F32)).astype(jnp.int32)
    local = ids - j * bus_count
    hit = (local >= 0) & (local < bus_count)
    upto = (iota((gens, gens), 1) <= iota((gens, gens), 0)).astype(BF16)
    rank = nn(upto, hit.astype(BF16)) - 1.0
    rank = jnp.where(hit, rank, 512.0)
    local = jnp.where(hit, local, 0)
    spread = (iota((buses_n, width), 1) // slots == iota((buses_n, width), 0)).astype(BF16)
    rank_wide = nn(rank.astype(BF16), spread)
    high_wide = nn((local // 128).astype(BF16), spread)
    low_wide = nn((local % 128).astype(BF16), spread)
    taken = rank_wide == (iota((gens, width), 1) % slots).astype(F32)
    slot_bus = jnp.sum(jnp.where(taken, high_wide * 128.0 + low_wide + 1.0, 0.0), axis=0, keepdims=True)
    slot_bus = to_column(slot_bus).astype(jnp.int32) - 1
    slot_hit = (iota((width, bus_count), 1) == slot_bus).astype(BF16)
    stor_column = to_column(stor_bus[...].astype(F32)).astype(jnp.int32)
    stor_hit = (iota((stors, bus_count), 1) == stor_column).astype(BF16)
    ptdf_copy.wait()
    tile = 128
    half = line_count // 2
    a_copies = [[], []]
    for h in range(2):

        def columns_step(t, carry):
            at = pl.multiple_of(t * tile, tile)
            block = ptdf[pl.ds(pl.multiple_of(h * half + t * tile, tile), tile), :]
            value = nt(slot_hit, block).astype(BF16)
            a_send[h, :, :, pl.ds(at, tile)] = value.reshape(buses_n, slots, tile)
            return carry

        lax.fori_loop(0, half // tile, columns_step, 0)
        for off in range(1, buses_n):
            to = lax.rem(j + off, buses_n)
            a_copies[h].append(
                go(
                    remote(
                        a_send.at[h, to],
                        a_recv.at[h, j],
                        a_sem.at[h, 0, off],
                        a_sem.at[h, 1, off],
                        (i, to),
                    )
                )
            )
        a_recv[h, j] = a_send[h, j]

    wide = max(tile, 2 * share)
    group = wide // (2 * share)

    def load_step(t, carry):
        at = pl.multiple_of(t * wide, wide)
        block = ptdf[pl.ds(at, wide), :]
        flow_block = nt(block, load_low[...]).reshape(group, 2, share, rows)
        stor_block = nt(block, stor_hit)
        a_t[gens:, pl.ds(at, wide)] = stor_block.T.astype(BF16)
        stor_block = stor_block.astype(BF16).reshape(group, 2, share, stors)
        for w in range(2):
            load_flow[w, pl.ds(t * group, group)] = flow_block[:, w]
            a_n[w, pl.ds(t * group, group), :, gens:] = stor_block[:, w]
        return carry

    lax.fori_loop(0, line_count // wide, load_step, 0)
    own = jnp.sum(jnp.where(iota((gens, buses_n), 1) == j, ids, 0), axis=1, keepdims=True)
    target = own // bus_count
    target_hit = iota((gens, buses_n), 1) == target
    own_rank = nn(upto, target_hit.astype(BF16))
    own_rank = jnp.sum(jnp.where(target_hit, own_rank, 0.0), axis=1, keepdims=True).astype(jnp.int32) - 1
    place = (iota((gens, width), 1) == target * slots + own_rank).astype(BF16)
    back = nn(later, omega_in[...], HIGHEST)

    gather = [gather_forward(0, n, gather[n]) for n in range(chunks)]
    for h in range(2):
        for copy in a_copies[h]:
            copy.wait_recv()

        def place_step(t, carry):
            at = pl.multiple_of(t * wide, wide)
            start = pl.multiple_of(h * half + t * wide, wide)
            block = nn(place, a_recv[h, :, :, pl.ds(at, wide)].reshape(width, wide))
            a_t[:gens, pl.ds(start, wide)] = block.astype(BF16)
            block = block.T.astype(BF16).reshape(group, 2, share, gens)
            for w in range(2):
                a_n[w, pl.ds(h * (half // (2 * share)) + t * group, group), :, :gens] = block[:, w]
            return carry

        lax.fori_loop(0, half // wide, place_step, 0)

    total_units = units * buses_n
    pending = {}
    hold = {"omega": omega_in[...], "back": back, "mu": [mu[:, cut(n)] for n in range(chunks)]}
    gen_hist = {(0, n): gen_start[cut(n), :] for n in range(chunks)}
    stor_hist = {(0, n): stor_start[cut(n), :] for n in range(chunks)}

    def price_stage(k, n):
        for copy in gather[n]:
            copy.wait_recv()
        duals = dual_all[k, n].reshape(line_count, chunk)
        copies = []
        for off in range(1, lines_n + 1):
            to = lax.rem(i + off, lines_n)
            at = pl.multiple_of(to * piece, piece)
            value = nn(a_t[pl.ds(at, piece), :], duals)
            if off == lines_n:
                break
            price_part[k, n, off] = value.astype(BF16)
            copies.append(
                go(
                    remote(
                        price_part.at[k, n, off],
                        price_recv.at[k, n, off],
                        pr_sem.at[k, n, 0, off],
                        pr_sem.at[k, n, 1, off],
                        (to, j),
                    )
                )
            )
        pending[n] = (value, copies)

    def share_stage(k, n):
        total, copies = pending[n]
        for off in range(1, lines_n):
            copies[off - 1].wait_recv()
            total = total + price_recv[k, n, off].astype(F32)
        price_all[k, n, i] = total.astype(BF16)
        copies = []
        for off in range(1, lines_n):
            copies.append(
                go(
                    remote(
                        price_all.at[k, n, i],
                        price_all.at[k, n, i],
                        pg_sem.at[k, n, 0, off],
                        pg_sem.at[k, n, 1, off],
                        (lax.rem(i + off, lines_n), j),
                    )
                )
            )
        pending[n] = copies

    bal_copies = {}

    def take_balance(k, n):
        for copy in bal_copies[n]:
            copy.wait_recv()
        balance = bal_recv[k, n, 0]
        for a in range(1, buses_n):
            balance = balance + bal_recv[k, n, a]
        lam[n] = lam[n] + (KAPPA / total_units) * to_column(balance)

    def update_stage(k, n):
        gen_now, stor_now = (gen_hist[k, n], stor_hist[k, n])
        if k == 0:
            gen_mid, stor_mid = (gen_now, stor_now)
        else:
            take_balance(k - 1, n)
            gen_mid = gen_now + THETA * (gen_now - gen_hist[k - 1, n])
            stor_mid = stor_now + THETA * (stor_now - stor_hist[k - 1, n])
        for copy in pending[n]:
            copy.wait_recv()
        price = price_all[k, n].reshape(units, chunk).astype(F32).T
        gen_grad = 2.0 * gen_quad[...] * gen_mid + gen_lin[...] + lam[n] + price[:, :gens]
        gen_next = jnp.clip(gen_mid - TAU * gen_grad, 0.0, gen_max[...])
        stor_grad = 2.0 * stor_quad[...] * stor_mid + lam[n] + price[:, gens:] + hold["back"][cut(n), :]
        stor_next = jnp.clip(stor_mid - TAU * stor_grad, -stor_rate[...], stor_rate[...])
        gen_bar = 2.0 * gen_next - gen_now
        stor_bar = 2.0 * stor_next - stor_now
        bar_low = jnp.concatenate([gen_bar.astype(BF16), stor_bar.astype(BF16)], axis=1)

        def flow_half(w):
            value = nt(a_n[w].reshape(chips * share, units), bar_low)
            value = value.reshape(chips, share, chunk) - load_flow[w, :, :, cut(n)]
            flow_part[k, n, w] = value.astype(BF16)

        flow_half(1 - c)
        pending[n] = go(
            remote(
                flow_part.at[k, n, 1 - c],
                pair_recv.at[k, n],
                pair_sem.at[k, n, 0],
                pair_sem.at[k, n, 1],
                partner,
            )
        )
        flow_half(c)
        balance = (
            jnp.sum(gen_bar, axis=1, keepdims=True)
            + jnp.sum(stor_bar, axis=1, keepdims=True)
            - load_total[cut(n), :]
        )
        balance = to_row(balance)
        bal_send[k, n] = balance
        bal_recv[k, n, j] = balance
        bal_copies[n] = []
        for off in range(1, buses_n):
            bal_copies[n].append(
                go(
                    remote(
                        bal_send.at[k, n],
                        bal_recv.at[k, n, j],
                        bal_sem.at[k, n, 0, off],
                        bal_sem.at[k, n, 1, off],
                        (i, lax.rem(j + off, buses_n)),
                    )
                )
            )
        if k == 0:
            gen_keep[cut(n), :] = gen_next
            stor_keep[cut(n), :] = stor_next
            gen_hist[1, n] = gen_next
            stor_hist[1, n] = stor_next
        else:
            gen_out[cut(n), :] = gen_next
            stor_out[cut(n), :] = stor_next
        bar_keep[cut(n), :] = stor_bar

    def pair_stage(k, n):
        pending[n].wait_recv()
        copies = []
        for off in range(1, chips):
            to = lax.rem(z + off, chips)
            value = flow_part[k, n, c, to].astype(F32) + pair_recv[k, n, to].astype(F32)
            line_part[k, n, off] = value.astype(BF16)
            copies.append(
                go(
                    remote(
                        line_part.at[k, n, off],
                        line_recv.at[k, n, off],
                        line_sem.at[k, n, 0, off],
                        line_sem.at[k, n, 1, off],
                        (i, to * 2 + c),
                    )
                )
            )
        pending[n] = copies
        if n == chunks - 1:
            charge = nn(earlier, bar_keep[...], HIGHEST)
            shifted = hold["omega"] + SIGMA_STORE * charge
            omega = shifted - SIGMA_STORE * jnp.clip(shifted / SIGMA_STORE, -high_bound, high_bound)
            if k == 0:
                hold["omega"] = omega
                hold["back"] = nn(later, omega, HIGHEST)
            else:
                omega_out[...] = omega

    def dual_stage(k, n):
        flow = flow_part[k, n, c, z].astype(F32) + pair_recv[k, n, z].astype(F32)
        for off in range(1, chips):
            pending[n][off - 1].wait_recv()
            flow = flow + line_recv[k, n, off].astype(F32)
        shifted = hold["mu"][n] + SIGMA_FLOW * flow
        mu = shifted - SIGMA_FLOW * jnp.clip(shifted / SIGMA_FLOW, -limit, limit)
        if k == 0:
            hold["mu"][n] = mu
            dual_all[1, n, j] = mu.astype(BF16)
            gather[n] = gather_start(1, n)
        else:
            mu_out[cut(n), :] = flipped(mu)

    def forward_stage(k, n):
        gather[n] = gather_forward(k, n, gather[n])

    stages = []
    for k in range(2):
        if k:
            stages.append(functools.partial(forward_stage, k))
        for stage in (price_stage, share_stage, update_stage, pair_stage, dual_stage):
            stages.append(functools.partial(stage, k))
    for step in range(len(stages) + chunks - 1):
        for n in range(chunks):
            if 0 <= step - n < len(stages):
                stages[step - n](n)
    for n in range(chunks):
        take_balance(1, n)
    lam_out[...] = jnp.concatenate([to_row(lam[n]) for n in range(chunks)], axis=1)
    for copy in started:
        copy.wait_send()


def finish(*refs):
    count = len(refs) // 2
    for source, result in zip(refs[:count], refs[count:]):
        result[...] = source[...].reshape(result.shape)


def shards(
    ptdf,
    load,
    ratings,
    line_index,
    gen_bus,
    gen_quad,
    gen_lin,
    gen_max,
    gen_start,
    stor_bus,
    stor_quad,
    stor_rate,
    stor_energy,
    stor_start,
    lam_start,
    mu_start,
    omega_start,
):
    lines_n = lax.axis_size("lines")
    buses_n = lax.axis_size("buses")
    rows, bus_count = load.shape
    line_count = ptdf.shape[0]
    gens = gen_bus.shape[0]
    stors = stor_bus.shape[0]
    units = gens + stors
    share = line_count // buses_n
    chips = buses_n // 2
    piece = units // lines_n
    slots = max(8, (gens + buses_n - 1) // buses_n)
    slots = (slots + 15) // 16 * 16
    chunk = 128 if rows % 128 == 0 else rows
    chunks = rows // chunk
    vmem = pl.BlockSpec(memory_space=pltpu.VMEM)
    hbm = pl.BlockSpec(memory_space=pl.ANY)
    dma = pltpu.SemaphoreType.DMA
    outs = pl.pallas_call(
        functools.partial(kernel, lines_n, buses_n, slots),
        out_shape=(
            jax.ShapeDtypeStruct((rows, gens), F32),
            jax.ShapeDtypeStruct((rows, stors), F32),
            jax.ShapeDtypeStruct((1, rows), F32),
            jax.ShapeDtypeStruct((rows, share), F32),
            jax.ShapeDtypeStruct((rows, stors), F32),
        ),
        in_specs=[vmem] * 15 + [hbm] * 2,
        out_specs=(vmem,) * 5,
        scratch_shapes=[
            pltpu.VMEM((line_count, bus_count), BF16),
            pltpu.VMEM((rows, bus_count), F32),
            pltpu.VMEM((rows, bus_count), BF16),
            pltpu.VMEM((2, chips, share, rows), F32),
            pltpu.VMEM((buses_n, 1, gens), jnp.int32),
            pltpu.VMEM((2, buses_n, slots, line_count // 2), BF16),
            pltpu.VMEM((2, buses_n, slots, line_count // 2), BF16),
            pltpu.VMEM((units, line_count), BF16),
            pltpu.VMEM((2, chips, share, units), BF16),
            pltpu.VMEM((2, chunks, buses_n, share, chunk), BF16),
            pltpu.VMEM((2, chunks, lines_n, piece, chunk), BF16),
            pltpu.VMEM((2, chunks, lines_n, piece, chunk), BF16),
            pltpu.VMEM((2, chunks, lines_n, piece, chunk), BF16),
            pltpu.VMEM((rows, gens), F32),
            pltpu.VMEM((rows, stors), F32),
            pltpu.VMEM((rows, stors), F32),
            pltpu.VMEM((2, chunks, 2, chips, share, chunk), BF16),
            pltpu.VMEM((2, chunks, chips, share, chunk), BF16),
            pltpu.VMEM((2, chunks, chips, share, chunk), BF16),
            pltpu.VMEM((2, chunks, chips, share, chunk), BF16),
            pltpu.VMEM((2, chunks, 1, chunk), F32),
            pltpu.VMEM((2, chunks, buses_n, 1, chunk), F32),
            dma((2,)),
            dma((2, buses_n)),
            dma((2, 2, buses_n)),
            dma((2, chunks, 2, chips)),
            dma((2, chunks, 2, chips)),
            dma((2, chunks, 2, lines_n)),
            dma((2, chunks, 2, lines_n)),
            dma((2, chunks, 2)),
            dma((2, chunks, 2, chips)),
            dma((2, chunks, 2, buses_n)),
        ],
        compiler_params=pltpu.CompilerParams(
            collective_id=0, has_side_effects=True, vmem_limit_bytes=60 * 1024 * 1024
        ),
    )(
        gen_bus[None, :],
        mu_start,
        ratings.reshape(-1, 128),
        line_index.reshape(buses_n, share),
        gen_quad[None, :],
        gen_lin[None, :],
        gen_max[None, :],
        gen_start,
        stor_bus[None, :],
        stor_quad[None, :],
        stor_rate[None, :],
        stor_energy[None, :],
        stor_start,
        lam_start,
        omega_start,
        ptdf,
        load,
    )
    shapes = [x.shape for x in outs]
    shapes[2] = (rows,)
    return pl.pallas_call(
        finish,
        out_shape=tuple(jax.ShapeDtypeStruct(shape, F32) for shape in shapes),
        in_specs=[vmem] * 5,
        out_specs=(vmem,) * 5,
    )(*outs)


def solution(mesh):
    return jax.shard_map(
        shards,
        mesh=mesh,
        in_specs=(
            P("lines", "buses"),
            P(None, "buses"),
            P(),
            P("lines"),
            P("buses"),
            P("buses"),
            P("buses"),
            P("buses"),
            P(None, "buses"),
            P("buses"),
            P("buses"),
            P("buses"),
            P("buses"),
            P(None, "buses"),
            P(),
            P(None, ("lines", "buses")),
            P(None, "buses"),
        ),
        out_specs=(
            P(None, "buses"),
            P(None, "buses"),
            P(),
            P(None, ("lines", "buses")),
            P(None, "buses"),
        ),
        check_vma=False,
    )
```

```python
import functools
import jax
import jax.numpy as jnp
from jax import lax
from jax.experimental import pallas as pl
from jax.experimental.pallas import tpu as pltpu
from jax.sharding import PartitionSpec as P

HOURS = 24
TAU = 0.25
SIGMA_FLOW = 4.0
SIGMA_STORE = 0.25
KAPPA = 1.0
THETA = 0.5

F32 = jnp.float32
BF16 = jnp.bfloat16
MESH = pl.DeviceIdType.MESH
HIGHEST = lax.Precision.HIGHEST


def nt(a, b, precision=None):
    return lax.dot_general(
        a, b, (((1,), (1,)), ((), ())), preferred_element_type=F32, precision=precision
    )


def nn(a, b, precision=None):
    return lax.dot_general(
        a, b, (((1,), (0,)), ((), ())), preferred_element_type=F32, precision=precision
    )


def iota(shape, dim):
    return lax.broadcasted_iota(jnp.int32, shape, dim)


def eye(n):
    return iota((n, n), 0) == iota((n, n), 1)


def masked_sum(mask, x):
    high = x.astype(BF16)
    rest = x - high.astype(F32)
    mid = rest.astype(BF16)
    low = (rest - mid.astype(F32)).astype(BF16)
    mask = mask.astype(BF16)
    return nn(mask, high) + (nn(mask, mid) + nn(mask, low))


def flipped(x):
    if x.shape[0] % 128 == 0 and x.shape[1] % 128 == 0:
        return x.T
    return nt(eye(x.shape[1]).astype(F32), x, HIGHEST)


def to_column(row):
    n = row.shape[1]
    return jnp.sum(jnp.where(eye(n), row, 0.0), axis=1, keepdims=True)


def to_row(column):
    n = column.shape[0]
    return jnp.sum(jnp.where(eye(n), column, 0.0), axis=0, keepdims=True)


def remote(src, dst, send_sem, recv_sem, target):
    return pltpu.make_async_remote_copy(
        src_ref=src,
        dst_ref=dst,
        send_sem=send_sem,
        recv_sem=recv_sem,
        device_id=target,
        device_id_type=MESH,
    )


def kernel(
    lines_n,
    buses_n,
    slots,
    gen_bus,
    mu_in_hbm,
    ratings_hbm,
    line_index,
    gen_quad,
    gen_lin,
    gen_max,
    gen_start_hbm,
    stor_bus,
    stor_quad,
    stor_rate,
    stor_energy,
    stor_start_hbm,
    lam_in,
    omega_in_hbm,
    ptdf_hbm,
    load_hbm,
    gen_out,
    stor_out,
    lam_out,
    mu_out,
    omega_out,
    ptdf,
    load,
    load_low,
    load_flow,
    gen_all,
    a_send,
    a_recv,
    a_t,
    a_n,
    dual_all,
    price_part,
    price_recv,
    price_all,
    gen_keep,
    stor_keep,
    bar_keep,
    flow_part,
    pair_recv,
    line_part,
    line_recv,
    bal_send,
    bal_recv,
    gen_start,
    stor_start,
    omega_in,
    mu_in,
    ratings,
    in_sem,
    idx_sem,
    a_sem,
    ag_sem,
    fwd_sem,
    pr_sem,
    pg_sem,
    pair_sem,
    line_sem,
    bal_sem,
):
    rows = load.shape[0]
    line_count, bus_count = ptdf.shape
    gens = gen_bus.shape[1]
    stors = stor_bus.shape[1]
    units = gens + stors
    share = mu_in.shape[1]
    chips = buses_n // 2
    width = buses_n * slots
    piece = units // lines_n
    i = lax.axis_index("lines")
    j = lax.axis_index("buses")
    z = j // 2
    c = j % 2
    partner = (i, z * 2 + (1 - c))
    chunk = dual_all.shape[-1]
    chunks = rows // chunk

    def cut(n):
        return slice(n * chunk, (n + 1) * chunk)


    load_copy = pltpu.make_async_copy(load_hbm, load, in_sem.at[0])
    ptdf_copy = pltpu.make_async_copy(ptdf_hbm, ptdf, in_sem.at[1])
    small_copies = [
        pltpu.make_async_copy(source, into, in_sem.at[2 + n])
        for n, (source, into) in enumerate(
            (
                (mu_in_hbm, mu_in),
                (ratings_hbm, ratings),
                (gen_start_hbm, gen_start),
                (stor_start_hbm, stor_start),
                (omega_in_hbm, omega_in),
            )
        )
    ]
    for copy in small_copies:
        copy.start()
    ptdf_copy.start()
    load_copy.start()

    barrier = pltpu.get_barrier_semaphore()
    for off in range(1, buses_n):
        pl.semaphore_signal(
            barrier, inc=1, device_id=(i, lax.rem(j + off, buses_n)), device_id_type=MESH
        )
    for off in range(1, lines_n):
        pl.semaphore_signal(
            barrier, inc=1, device_id=(lax.rem(i + off, lines_n), j), device_id_type=MESH
        )

    gen_all[j] = gen_bus[...]
    small_copies[0].wait()
    mu = flipped(mu_in[...])
    for n in range(chunks):
        dual_all[0, n, j] = mu[:, cut(n)].astype(BF16)
    pl.semaphore_wait(barrier, buses_n + lines_n - 2)

    started = []

    def go(copy):
        copy.start()
        started.append(copy)
        return copy

    idx_copies = []
    for off in range(1, buses_n):
        idx_copies.append(
            go(
                remote(
                    gen_bus,
                    gen_all.at[j],
                    idx_sem.at[0, off],
                    idx_sem.at[1, off],
                    (i, lax.rem(j + off, buses_n)),
                )
            )
        )

    def gather_start(k, n):
        mine = dual_all.at[k, n, j]
        copies = []
        for off in range(1, chips):
            copies.append(
                go(
                    remote(
                        mine,
                        mine,
                        ag_sem.at[k, n, 0, off],
                        ag_sem.at[k, n, 1, off],
                        (i, lax.rem(z + off, chips) * 2 + c),
                    )
                )
            )
        copies.append(go(remote(mine, mine, ag_sem.at[k, n, 0, 0], ag_sem.at[k, n, 1, 0], partner)))
        return copies

    def gather_forward(k, n, copies):
        forwards = [copies[-1]]
        for off in range(1, chips):
            copies[off - 1].wait_recv()
            slot = dual_all.at[k, n, lax.rem(z - off + chips, chips) * 2 + c]
            forwards.append(
                go(remote(slot, slot, fwd_sem.at[k, n, 0, off], fwd_sem.at[k, n, 1, off], partner))
            )
        return forwards

    gather = [gather_start(0, n) for n in range(chunks)]

    for copy in idx_copies:
        copy.wait_recv()
    ids = jnp.concatenate([gen_all[a] for a in range(buses_n)], axis=0)
    ids = ids.astype(F32).T.astype(jnp.int32)
    local = ids - j * bus_count
    hit = (local >= 0) & (local < bus_count)
    upto = (iota((gens, gens), 1) <= iota((gens, gens), 0)).astype(BF16)
    rank = nn(upto, hit.astype(BF16)) - 1.0
    rank = jnp.where(hit, rank, 512.0)
    local = jnp.where(hit, local, 0)
    spread = (iota((buses_n, width), 1) // slots == iota((buses_n, width), 0)).astype(BF16)
    rank_wide = nn(rank.astype(BF16), spread)
    high_wide = nn((local // 128).astype(BF16), spread)
    low_wide = nn((local % 128).astype(BF16), spread)
    taken = rank_wide == (iota((gens, width), 1) % slots).astype(F32)
    slot_bus = jnp.sum(jnp.where(taken, high_wide * 128.0 + low_wide + 1.0, 0.0), axis=0, keepdims=True)
    slot_bus = to_column(slot_bus).astype(jnp.int32) - 1
    slot_hit = (iota((width, bus_count), 1) == slot_bus).astype(BF16)
    ptdf_copy.wait()
    tile = 256 if line_count % 512 == 0 else 128
    half = line_count // 2
    a_copies = [[], []]
    for h in range(2):

        def columns_step(t, carry):
            at = pl.multiple_of(t * tile, tile)
            block = ptdf[pl.ds(pl.multiple_of(h * half + t * tile, tile), tile), :]
            value = nt(slot_hit, block).astype(BF16)
            a_send[h, :, :, pl.ds(at, tile)] = value.reshape(buses_n, slots, tile)
            return carry

        lax.fori_loop(0, half // tile, columns_step, 0)
        for off in range(1, buses_n):
            to = lax.rem(j + off, buses_n)
            a_copies[h].append(
                go(
                    remote(
                        a_send.at[h, to],
                        a_recv.at[h, j],
                        a_sem.at[h, 0, off],
                        a_sem.at[h, 1, off],
                        (i, to),
                    )
                )
            )
        a_recv[h, j] = a_send[h, j]

    stor_column = to_column(stor_bus[...].astype(F32)).astype(jnp.int32)
    stor_hit = (iota((stors, bus_count), 1) == stor_column).astype(BF16)
    for copy in small_copies[1:]:
        copy.wait()
    load_copy.wait()
    load_value = load[...]
    load_total = jnp.sum(load_value, axis=1, keepdims=True)
    load_low[...] = load_value.astype(BF16)
    lam_row = lam_in[...].reshape(1, rows)
    lam = [to_column(lam_row[:, cut(n)]) for n in range(chunks)]
    wanted = jnp.sum(
        jnp.where(iota((buses_n, share), 0) == j, line_index[...].astype(F32), 0.0),
        axis=0,
        keepdims=True,
    )
    wanted = to_column(wanted).astype(jnp.int32)
    lanes = ratings.shape[1]
    high_hit = (iota((share, ratings.shape[0]), 1) == wanted // lanes).astype(F32)
    rated = masked_sum(high_hit, ratings[...])
    limit = jnp.sum(
        jnp.where(iota((share, lanes), 1) == wanted % lanes, rated, 0.0), axis=1, keepdims=True
    )
    hour = iota((rows, 1), 0) % HOURS
    half_energy = 0.5 * stor_energy[...]
    high_bound = jnp.where(hour == HOURS - 1, 0.0, half_energy)
    row_id, col_id = (iota((rows, rows), 0), iota((rows, rows), 1))
    same = row_id // HOURS == col_id // HOURS
    later = jnp.where(same & (col_id >= row_id), 1.0, 0.0)
    earlier = jnp.where(same & (col_id <= row_id), 1.0, 0.0)

    wide = max(128, 2 * share)
    group = wide // (2 * share)

    def load_step(t, carry):
        at = pl.multiple_of(t * wide, wide)
        block = ptdf[pl.ds(at, wide), :]
        flow_block = nt(block, load_low[...]).reshape(group, 2, share, rows)
        stor_block = nt(block, stor_hit)
        a_t[gens:, pl.ds(at, wide)] = stor_block.T.astype(BF16)
        stor_block = stor_block.astype(BF16).reshape(group, 2, share, stors)
        for w in range(2):
            load_flow[w, pl.ds(t * group, group)] = flow_block[:, w]
            a_n[w, pl.ds(t * group, group), :, gens:] = stor_block[:, w]
        return carry

    lax.fori_loop(0, line_count // wide, load_step, 0)
    own = jnp.sum(jnp.where(iota((gens, buses_n), 1) == j, ids, 0), axis=1, keepdims=True)
    target = own // bus_count
    target_hit = iota((gens, buses_n), 1) == target
    own_rank = nn(upto, target_hit.astype(BF16))
    own_rank = jnp.sum(jnp.where(target_hit, own_rank, 0.0), axis=1, keepdims=True).astype(jnp.int32) - 1
    place = (iota((gens, width), 1) == target * slots + own_rank).astype(BF16)
    back = masked_sum(later, omega_in[...])

    gather = [gather_forward(0, n, gather[n]) for n in range(chunks)]
    for h in range(2):
        for copy in a_copies[h]:
            copy.wait_recv()

        def place_step(t, carry):
            at = pl.multiple_of(t * wide, wide)
            start = pl.multiple_of(h * half + t * wide, wide)
            block = nn(place, a_recv[h, :, :, pl.ds(at, wide)].reshape(width, wide))
            a_t[:gens, pl.ds(start, wide)] = block.astype(BF16)
            block = block.T.astype(BF16).reshape(group, 2, share, gens)
            for w in range(2):
                a_n[w, pl.ds(h * (half // (2 * share)) + t * group, group), :, :gens] = block[:, w]
            return carry

        lax.fori_loop(0, half // wide, place_step, 0)

    total_units = units * buses_n
    pending = {}
    hold = {"omega": omega_in[...], "back": back, "mu": [mu[:, cut(n)] for n in range(chunks)]}
    gen_hist = {(0, n): gen_start[cut(n), :] for n in range(chunks)}
    stor_hist = {(0, n): stor_start[cut(n), :] for n in range(chunks)}

    def price_stage(k, n):
        for copy in gather[n]:
            copy.wait_recv()
        duals = dual_all[k, n].reshape(line_count, chunk)
        value = nn(a_t[...], duals).reshape(lines_n, piece, chunk)
        price_part[k, n] = value.astype(BF16)
        copies = []
        for off in range(1, lines_n):
            to = lax.rem(i + off, lines_n)
            copies.append(
                go(
                    remote(
                        price_part.at[k, n, to],
                        price_recv.at[k, n, off],
                        pr_sem.at[k, n, 0, off],
                        pr_sem.at[k, n, 1, off],
                        (to, j),
                    )
                )
            )
        pending[n] = copies

    def share_stage(k, n):
        copies = pending[n]
        total = price_part[k, n, i].astype(F32)
        for off in range(1, lines_n):
            copies[off - 1].wait_recv()
            total = total + price_recv[k, n, off].astype(F32)
        price_all[k, n, i] = total.astype(BF16)
        copies = []
        for off in range(1, lines_n):
            copies.append(
                go(
                    remote(
                        price_all.at[k, n, i],
                        price_all.at[k, n, i],
                        pg_sem.at[k, n, 0, off],
                        pg_sem.at[k, n, 1, off],
                        (lax.rem(i + off, lines_n), j),
                    )
                )
            )
        pending[n] = copies

    bal_copies = {}

    def take_balance(k, n):
        for copy in bal_copies[n]:
            copy.wait_recv()
        balance = bal_recv[k, n, 0]
        for a in range(1, buses_n):
            balance = balance + bal_recv[k, n, a]
        lam[n] = lam[n] + (KAPPA / total_units) * to_column(balance)

    def update_stage(k, n):
        gen_now, stor_now = (gen_hist[k, n], stor_hist[k, n])
        if k == 0:
            gen_mid, stor_mid = (gen_now, stor_now)
        else:
            take_balance(k - 1, n)
            gen_mid = gen_now + THETA * (gen_now - gen_hist[k - 1, n])
            stor_mid = stor_now + THETA * (stor_now - stor_hist[k - 1, n])
        for copy in pending[n]:
            copy.wait_recv()
        price = price_all[k, n].reshape(units, chunk).astype(F32).T
        gen_grad = 2.0 * gen_quad[...] * gen_mid + gen_lin[...] + lam[n] + price[:, :gens]
        gen_next = jnp.clip(gen_mid - TAU * gen_grad, 0.0, gen_max[...])
        stor_grad = 2.0 * stor_quad[...] * stor_mid + lam[n] + price[:, gens:] + hold["back"][cut(n), :]
        stor_next = jnp.clip(stor_mid - TAU * stor_grad, -stor_rate[...], stor_rate[...])
        gen_bar = 2.0 * gen_next - gen_now
        stor_bar = 2.0 * stor_next - stor_now
        bar_low = jnp.concatenate([gen_bar.astype(BF16), stor_bar.astype(BF16)], axis=1)

        def flow_half(w):
            value = nt(a_n[w].reshape(chips * share, units), bar_low)
            value = value.reshape(chips, share, chunk) - load_flow[w, :, :, cut(n)]
            flow_part[k, n, w] = value.astype(BF16)

        flow_half(1 - c)
        pending[n] = go(
            remote(
                flow_part.at[k, n, 1 - c],
                pair_recv.at[k, n],
                pair_sem.at[k, n, 0],
                pair_sem.at[k, n, 1],
                partner,
            )
        )
        flow_half(c)
        balance = (
            jnp.sum(gen_bar, axis=1, keepdims=True)
            + jnp.sum(stor_bar, axis=1, keepdims=True)
            - load_total[cut(n), :]
        )
        balance = to_row(balance)
        bal_send[k, n] = balance
        bal_recv[k, n, j] = balance
        bal_copies[n] = []
        for off in range(1, buses_n):
            bal_copies[n].append(
                go(
                    remote(
                        bal_send.at[k, n],
                        bal_recv.at[k, n, j],
                        bal_sem.at[k, n, 0, off],
                        bal_sem.at[k, n, 1, off],
                        (i, lax.rem(j + off, buses_n)),
                    )
                )
            )
        if k == 0:
            gen_keep[cut(n), :] = gen_next
            stor_keep[cut(n), :] = stor_next
            gen_hist[1, n] = gen_next
            stor_hist[1, n] = stor_next
        else:
            gen_out[cut(n), :] = gen_next
            stor_out[cut(n), :] = stor_next
        bar_keep[cut(n), :] = stor_bar

    def pair_stage(k, n):
        pending[n].wait_recv()
        copies = []
        for off in range(1, chips):
            to = lax.rem(z + off, chips)
            value = flow_part[k, n, c, to].astype(F32) + pair_recv[k, n, to].astype(F32)
            line_part[k, n, off] = value.astype(BF16)
            copies.append(
                go(
                    remote(
                        line_part.at[k, n, off],
                        line_recv.at[k, n, off],
                        line_sem.at[k, n, 0, off],
                        line_sem.at[k, n, 1, off],
                        (i, to * 2 + c),
                    )
                )
            )
        pending[n] = copies
        if n == chunks - 1:
            charge = masked_sum(earlier, bar_keep[...])
            shifted = hold["omega"] + SIGMA_STORE * charge
            omega = shifted - SIGMA_STORE * jnp.clip(shifted / SIGMA_STORE, -high_bound, high_bound)
            if k == 0:
                hold["omega"] = omega
                hold["back"] = masked_sum(later, omega)
            else:
                omega_out[...] = omega

    def dual_stage(k, n):
        flow = flow_part[k, n, c, z].astype(F32) + pair_recv[k, n, z].astype(F32)
        for off in range(1, chips):
            pending[n][off - 1].wait_recv()
            flow = flow + line_recv[k, n, off].astype(F32)
        shifted = hold["mu"][n] + SIGMA_FLOW * flow
        mu = shifted - SIGMA_FLOW * jnp.clip(shifted / SIGMA_FLOW, -limit, limit)
        if k == 0:
            hold["mu"][n] = mu
            dual_all[1, n, j] = mu.astype(BF16)
            gather[n] = gather_start(1, n)
        else:
            mu_out[cut(n), :] = flipped(mu)

    def forward_stage(k, n):
        gather[n] = gather_forward(k, n, gather[n])

    stages = []
    for k in range(2):
        if k:
            stages.append(functools.partial(forward_stage, k))
        for stage in (price_stage, share_stage, update_stage, pair_stage, dual_stage):
            stages.append(functools.partial(stage, k))
    for step in range(len(stages) + chunks - 1):
        for n in range(chunks):
            if 0 <= step - n < len(stages):
                stages[step - n](n)
    for n in range(chunks):
        take_balance(1, n)
    lam_out[...] = jnp.concatenate([to_row(lam[n]) for n in range(chunks)], axis=1)
    for copy in started:
        copy.wait_send()


def finish(*refs):
    count = len(refs) // 2
    for source, result in zip(refs[:count], refs[count:]):
        result[...] = source[...].reshape(result.shape)


def shards(
    ptdf,
    load,
    ratings,
    line_index,
    gen_bus,
    gen_quad,
    gen_lin,
    gen_max,
    gen_start,
    stor_bus,
    stor_quad,
    stor_rate,
    stor_energy,
    stor_start,
    lam_start,
    mu_start,
    omega_start,
):
    lines_n = lax.axis_size("lines")
    buses_n = lax.axis_size("buses")
    rows, bus_count = load.shape
    line_count = ptdf.shape[0]
    gens = gen_bus.shape[0]
    stors = stor_bus.shape[0]
    units = gens + stors
    share = line_count // buses_n
    chips = buses_n // 2
    piece = units // lines_n
    slots = max(8, (gens + buses_n - 1) // buses_n)
    slots = (slots + 15) // 16 * 16
    chunk = 128 if rows % 128 == 0 else rows
    chunks = rows // chunk
    vmem = pl.BlockSpec(memory_space=pltpu.VMEM)
    hbm = pl.BlockSpec(memory_space=pl.ANY)
    dma = pltpu.SemaphoreType.DMA
    outs = pl.pallas_call(
        functools.partial(kernel, lines_n, buses_n, slots),
        out_shape=(
            jax.ShapeDtypeStruct((rows, gens), F32),
            jax.ShapeDtypeStruct((rows, stors), F32),
            jax.ShapeDtypeStruct((1, rows), F32),
            jax.ShapeDtypeStruct((rows, share), F32),
            jax.ShapeDtypeStruct((rows, stors), F32),
        ),
        in_specs=[hbm if n in (1, 2, 7, 12, 14, 15, 16) else vmem for n in range(17)],
        out_specs=(vmem,) * 5,
        scratch_shapes=[
            pltpu.VMEM((line_count, bus_count), BF16),
            pltpu.VMEM((rows, bus_count), F32),
            pltpu.VMEM((rows, bus_count), BF16),
            pltpu.VMEM((2, chips, share, rows), F32),
            pltpu.VMEM((buses_n, 1, gens), jnp.int32),
            pltpu.VMEM((2, buses_n, slots, line_count // 2), BF16),
            pltpu.VMEM((2, buses_n, slots, line_count // 2), BF16),
            pltpu.VMEM((units, line_count), BF16),
            pltpu.VMEM((2, chips, share, units), BF16),
            pltpu.VMEM((2, chunks, buses_n, share, chunk), BF16),
            pltpu.VMEM((2, chunks, lines_n, piece, chunk), BF16),
            pltpu.VMEM((2, chunks, lines_n, piece, chunk), BF16),
            pltpu.VMEM((2, chunks, lines_n, piece, chunk), BF16),
            pltpu.VMEM((rows, gens), F32),
            pltpu.VMEM((rows, stors), F32),
            pltpu.VMEM((rows, stors), F32),
            pltpu.VMEM((2, chunks, 2, chips, share, chunk), BF16),
            pltpu.VMEM((2, chunks, chips, share, chunk), BF16),
            pltpu.VMEM((2, chunks, chips, share, chunk), BF16),
            pltpu.VMEM((2, chunks, chips, share, chunk), BF16),
            pltpu.VMEM((2, chunks, 1, chunk), F32),
            pltpu.VMEM((2, chunks, buses_n, 1, chunk), F32),
            pltpu.VMEM((rows, gens), F32),
            pltpu.VMEM((rows, stors), F32),
            pltpu.VMEM((rows, stors), F32),
            pltpu.VMEM((rows, share), F32),
            pltpu.VMEM((ratings.shape[0] // 128, 128), F32),
            dma((7,)),
            dma((2, buses_n)),
            dma((2, 2, buses_n)),
            dma((2, chunks, 2, chips)),
            dma((2, chunks, 2, chips)),
            dma((2, chunks, 2, lines_n)),
            dma((2, chunks, 2, lines_n)),
            dma((2, chunks, 2)),
            dma((2, chunks, 2, chips)),
            dma((2, chunks, 2, buses_n)),
        ],
        compiler_params=pltpu.CompilerParams(
            collective_id=0, has_side_effects=True, vmem_limit_bytes=60 * 1024 * 1024
        ),
    )(
        gen_bus[None, :],
        mu_start,
        ratings.reshape(-1, 128),
        line_index.reshape(buses_n, share),
        gen_quad[None, :],
        gen_lin[None, :],
        gen_max[None, :],
        gen_start,
        stor_bus[None, :],
        stor_quad[None, :],
        stor_rate[None, :],
        stor_energy[None, :],
        stor_start,
        lam_start,
        omega_start,
        ptdf,
        load,
    )
    shapes = [x.shape for x in outs]
    shapes[2] = (rows,)
    return pl.pallas_call(
        finish,
        out_shape=tuple(jax.ShapeDtypeStruct(shape, F32) for shape in shapes),
        in_specs=[vmem] * 5,
        out_specs=(vmem,) * 5,
    )(*outs)


def solution(mesh):
    return jax.shard_map(
        shards,
        mesh=mesh,
        in_specs=(
            P("lines", "buses"),
            P(None, "buses"),
            P(),
            P("lines"),
            P("buses"),
            P("buses"),
            P("buses"),
            P("buses"),
            P(None, "buses"),
            P("buses"),
            P("buses"),
            P("buses"),
            P("buses"),
            P(None, "buses"),
            P(),
            P(None, ("lines", "buses")),
            P(None, "buses"),
        ),
        out_specs=(
            P(None, "buses"),
            P(None, "buses"),
            P(),
            P(None, ("lines", "buses")),
            P(None, "buses"),
        ),
        check_vma=False,
    )
```
